32 devices in a mesh: dp: 4 (over z), seq: 8 (over y, x, core).
Axes of the slice: x: 2, y: 2, z: 4, core: 2. Of those that a mesh axis runs over, the one named last changes fastest.
Arguments:
- layer_input: bfloat16 [4, 1024, 2048], P('dp', 'seq'), may hold values from -6 to 6
- document_lengths: int32 [4, 4], P('dp'), may hold values from 1 to 512, 1024 in all within a row
- attention_gain: float32 [2048], replicated, may hold values from 0.5 to 1.5
- attention_in: bfloat16 [2048, 3072], P(('dp', 'seq')), may hold values from -0.125 to 0.125
- query_gain: float32 [64], replicated, may hold values from 0.5 to 1.5
- key_gain: float32 [64], replicated, may hold values from 0.5 to 1.5
- attention_out: bfloat16 [2048, 2048], P(('dp', 'seq')), may hold values from -1 to 1
- feed_gain: float32 [2048], replicated, may hold values from 0.5 to 1.5
- feed_weight: bfloat16 [8192, 6144], P(('dp', 'seq')), may hold values from -0.25 to 0.25
- cotangent: bfloat16 [4, 1024, 2048], P('dp', 'seq'), may hold values from -6 to 6
Outputs:
- layer_output: bfloat16 [4, 1024, 2048], P('dp', 'seq')
- input_gradient: bfloat16 [4, 1024, 2048], P('dp', 'seq')
- attention_gain_gradient: float32 [2048], replicated
- attention_in_gradient: float32 [2048, 3072], P(('dp', 'seq'))
- query_gain_gradient: float32 [64], replicated
- key_gain_gradient: float32 [64], replicated
- attention_out_gradient: float32 [2048, 2048], P(('dp', 'seq'))
- feed_gain_gradient: float32 [2048], replicated
- feed_weight_gradient: float32 [8192, 6144], P(('dp', 'seq'))
The draws below stay inside these ranges and needn't reach their ends.
Inputs may be any that keep to these rules, and one draw needn't show every extreme that they name: `document_lengths`: each row's 4 document lengths sum to 1024, and the longest of every row is exactly 512.
All inputs are finite; a program needn't handle non-finite values.
Results may differ from the reference program's by a relative error of at most 0.02.
Values may be sent and summed in bfloat16 or wider, within the bound.
No kernel may reach another device: no remote copies, remote signals or barrier semaphores. Data moves between devices by JAX's collectives and lax.ppermute only.
A program may use at most 832 MiB of HBM per device.

```python
import math
import jax
import jax.numpy as jnp
import numpy as np
from jax import lax

D = 2048
HEADS = 32
KV_HEADS = 8
HEAD_DIM = 64
FF = 8192
DOCS = 4
ROWS = 4
SEQ = 1024
QKV = 3072


def raised(array, rng, source, target, parts, factor):
    def block_of(position):
        return (jnp.arange(array.shape[position]) // (array.shape[position] // parts)).reshape((-1,) + (1,) * (array.ndim - 1 - position))

    one_side = jax.random.permutation(rng, parts)[block_of(target)]
    far = (block_of(target) + parts // 2) % parts
    return jnp.where((block_of(source) == one_side) | (block_of(source) == far), factor * array, array)


def level_of(key, extent, shards, smallest, top_value):
    level, own = 1.0, jax.random.fold_in(key, 6)
    for position, blocks in shards:
        heights = jnp.exp(jax.random.uniform(jax.random.fold_in(own, position), (blocks,), jnp.float32, smallest / len(shards), top_value / len(shards)))
        level = level * jnp.repeat(heights, extent[position] // blocks).reshape([-1 if axis == position else 1 for axis in range(len(extent))])
    return level


def length_profile(count, total, reach, skew):
    weights = [(1 << 20) // math.isqrt(rank ** skew) + 1 for rank in range(2, count + 1)]
    surplus, given = total - reach - (count - 1), [1] * (count - 1)
    while surplus > 0:
        candidates = [i for i in range(count - 1) if given[i] < reach]
        whole, left = sum([weights[i] for i in candidates]), surplus
        for i in candidates:
            addition = min(reach - given[i], max(1, left * weights[i] // whole), surplus)
            given[i] = given[i] + addition
            surplus = surplus - addition
    return np.array([reach] + given)


def uneven(key, amount, total, most, lean):
    if amount == 2:
        one = jax.random.randint(key, (), max(1, total - most), min(most, total - 1) + 1)
        return jnp.stack([one, total - one])
    sizes = jnp.asarray(length_profile(amount, total, most, lean), jnp.int32)
    pairs = (amount - 1) // 2
    giver, sink = sizes[1:1 + 2 * pairs:2], sizes[2:2 + 2 * pairs:2]
    room = jnp.minimum(giver - 1, most - sink)
    moved = jax.random.randint(jax.random.fold_in(key, 1), (pairs,), 0, 1 << 20) % (room + 1)
    sizes = sizes.at[1:1 + 2 * pairs:2].set(giver - moved).at[2:2 + 2 * pairs:2].set(sink + moved)
    return sizes[jax.random.permutation(jax.random.fold_in(key, 2), amount)]


def centred(stream_key, shape, spread, reach, pieces=(), held_as=jnp.bfloat16):
    entries = spread * jax.random.normal(stream_key, shape, jnp.float32)
    if pieces:
        entries = entries * level_of(stream_key, shape, pieces, -0.22, 0.18)
    return jnp.clip(entries, -reach, reach).astype(held_as)


def gaussian_with(rng, shape, spread, limit, split, heavy, held_as=jnp.bfloat16):
    entries = spread * jax.random.normal(rng, shape, jnp.float32)
    if split:
        entries = entries * level_of(rng, shape, split, -0.22, 0.18)
    return jnp.clip(raised(entries, jax.random.fold_in(rng, 3), *heavy), -limit, limit).astype(held_as)


def setup_inputs(seed: int = 0) -> dict:
    splits = jax.random.split(jax.random.key(seed), 11)
    return {
        "layer_input": centred(splits[0], (ROWS, SEQ, D), 1.0, 6.0, ((0, 4), (1, 8))),
        "document_lengths": jax.vmap(lambda own: uneven(own, DOCS, SEQ, SEQ // 2, 2))(jax.random.split(splits[1], ROWS)).reshape((ROWS, DOCS)).astype(jnp.int32),
        "attention_gain": jnp.clip(1.0 + 0.1 * jax.random.normal(splits[2], (D,), jnp.float32), 0.5, 1.5),
        "attention_in": centred(splits[3], (D, QKV), D ** -0.5, 0.125, ((0, 32),)),
        "query_gain": jnp.clip(1.0 + 0.1 * jax.random.normal(splits[4], (HEAD_DIM,), jnp.float32), 0.5, 1.5),
        "key_gain": jnp.clip(1.0 + 0.1 * jax.random.normal(splits[5], (HEAD_DIM,), jnp.float32), 0.5, 1.5),
        "attention_out": centred(splits[6], (D, D), (D // 64) ** -0.5, 1.0, ((0, 32),)),
        "feed_gain": jnp.clip(1.0 + 0.1 * jax.random.normal(splits[7], (D,), jnp.float32), 0.5, 1.5),
        "feed_weight": gaussian_with(splits[8], (FF, 3 * D), D ** -0.5, 0.25, ((0, 32),), (0, 1, 32, 2.75)),
        "cotangent": centred(splits[9], (ROWS, SEQ, D), 1.0, 6.0, ((0, 4), (1, 8))),
    }


EPSILON = 1e-06
NEGATIVE = -1e+30
PRECISE = lax.Precision.HIGHEST

@jax.custom_vjp
def low(v):
    return lax.optimization_barrier(v.astype(jnp.bfloat16)).astype(jnp.float32)

@jax.custom_vjp
def low_back(v):
    return v

def low_keep(v):
    return (low(v), None)

def low_pass(kept, grad):
    return (grad,)

def back_keep(v):
    return (v, None)

def back_low(kept, grad):
    return (low(grad),)
low.defvjp(low_keep, low_pass)
low_back.defvjp(back_keep, back_low)

def matmul(left, right):
    return jnp.dot(left, right, precision=PRECISE, preferred_element_type=jnp.float32)

def normalize(value, gain):
    return value * lax.rsqrt(lax.optimization_barrier(jnp.mean(value * value, axis=-1, keepdims=True)) + EPSILON) * gain

def rotate(value, angles):
    half = value.shape[-1] // 2
    cosine = jnp.cos(angles)[..., None, :]
    sine = jnp.sin(angles)[..., None, :]
    first = value[..., :half]
    second = value[..., half:]
    return jnp.concatenate([first * cosine - second * sine, second * cosine + first * sine], axis=-1)

def attend(query, keys, values, start_of):
    length = query.shape[0]
    block = min(512, length)
    key_place = jnp.arange(length).astype(jnp.int32)
    scale = HEAD_DIM ** (-0.5)

    def one_block(item):
        query_block, place_block, start_block = item
        scores = jnp.einsum('qgjd,kgd->gjqk', query_block, keys, precision=PRECISE, preferred_element_type=jnp.float32) * scale
        scores = low_back(scores)
        allowed = (key_place[None, :] <= place_block[:, None]) & (key_place[None, :] >= start_block[:, None])
        scores = jnp.where(allowed[None, None], scores, NEGATIVE)
        top = lax.optimization_barrier(jnp.max(scores, axis=-1, keepdims=True))
        expo = jnp.exp(scores - top)
        chance = low(expo / lax.optimization_barrier(jnp.sum(expo, axis=-1, keepdims=True)))
        return jnp.einsum('gjqk,kgd->qgjd', chance, values, precision=PRECISE, preferred_element_type=jnp.float32)
    count = length // block
    blocks = (query.reshape((count, block) + query.shape[1:]), key_place.reshape(count, block), start_of.astype(jnp.int32).reshape(count, block))
    result = lax.map(jax.checkpoint(one_block), blocks)
    return result.reshape(query.shape)

def row_forward(weights, sequence, start_of, angles):
    attention_gain, attention_in, query_gain, key_gain, attention_out, feed_gain, feed_weight = weights
    length = sequence.shape[0]
    split_key = D + KV_HEADS * HEAD_DIM
    normed = low(normalize(sequence, attention_gain))
    joined = low_back(matmul(normed, attention_in))
    query = joined[:, :D].reshape(length, HEADS, HEAD_DIM)
    keys = joined[:, D:split_key].reshape(length, KV_HEADS, HEAD_DIM)
    values = joined[:, split_key:].reshape(length, KV_HEADS, HEAD_DIM)
    query = low(rotate(normalize(query, query_gain), angles))
    keys = low(rotate(normalize(keys, key_gain), angles))
    values = low(values)
    attended = attend(query.reshape(length, KV_HEADS, HEADS // KV_HEADS, HEAD_DIM), keys, values, start_of)
    attended = low_back(low(attended.reshape(length, D)))
    branch = low_back(matmul(attended, attention_out))
    resid = sequence + branch
    normed_feed = low(normalize(resid, feed_gain))
    gate = low_back(matmul(normed_feed, feed_weight[:, :D].T))
    upward = low_back(matmul(normed_feed, feed_weight[:, D:2 * D].T))
    hidden = low(jax.nn.silu(gate) * upward)
    return resid + matmul(hidden, feed_weight[:, 2 * D:])

def reference(layer_input, document_lengths, attention_gain, attention_in, query_gain, key_gain, attention_out, feed_gain, feed_weight, cotangent):
    weights = tuple((item.astype(jnp.float32) for item in (attention_gain, attention_in, query_gain, key_gain, attention_out, feed_gain, feed_weight)))
    positions = jnp.arange(SEQ).astype(jnp.int32)
    half = HEAD_DIM // 2
    frequency = jnp.exp(jnp.arange(half).astype(jnp.float32) * (-2.0 * math.log(10000.0) / HEAD_DIM))

    def one_row(totals, item):
        sequence, lengths, row_cotangent = item
        lengths = lengths.astype(jnp.int32)
        ends = jnp.cumsum(lengths).astype(jnp.int32)
        start_of = lax.optimization_barrier(jnp.sum(jnp.where(positions[:, None] >= ends[None, :], lengths[None, :], 0), axis=1)).astype(jnp.int32)
        angles = (positions - start_of).astype(jnp.float32)[:, None] * frequency[None, :]
        result, pullback = jax.vjp(lambda wts, seqs: row_forward(wts, seqs, start_of, angles), weights, sequence.astype(jnp.float32))
        gradients, sequence_gradient = pullback(row_cotangent.astype(jnp.float32))
        totals = jax.tree.map(lambda left, right: left + right, totals, gradients)
        return (totals, (result.astype(jnp.bfloat16), sequence_gradient.astype(jnp.bfloat16)))
    empty = tuple((jnp.zeros(item.shape, jnp.float32) for item in weights))
    totals, (layer_output, input_gradient) = lax.scan(one_row, empty, (layer_input, document_lengths, cotangent))
    return (layer_output, input_gradient, totals[0], totals[1], totals[2], totals[3], totals[4], totals[5], totals[6])
```

```python
import functools
import math

import jax
import jax.numpy as jnp
import numpy as np
from jax import lax
from jax.experimental import pallas as pl
from jax.experimental.pallas import tpu as pltpu
from jax.sharding import PartitionSpec as P

D = 2048
HEADS = 32
KV_HEADS = 8
HEAD_DIM = 64
EPSILON = 1e-06
NEGATIVE = -1e30
AXES = ("dp", "seq")
CHUNKS = 2
F32 = jnp.float32
BF16 = jnp.bfloat16


def nt(left, right):
    return lax.dot_general(left, right, (((1,), (1,)), ((), ())), preferred_element_type=F32)


def nn(left, right):
    return jnp.dot(left, right, preferred_element_type=F32)


def tn(left, right):
    return lax.dot_general(left, right, (((0,), (0,)), ((), ())), preferred_element_type=F32)


def normalize(value, gain):
    return value * lax.rsqrt(jnp.mean(value * value, axis=-1, keepdims=True) + EPSILON) * gain


def rotate(value, cosine, sine):
    half = value.shape[-1] // 2
    first = value[..., :half]
    second = value[..., half:]
    return jnp.concatenate(
        [first * cosine - second * sine, second * cosine + first * sine], axis=-1
    )


class Links:
    def __init__(self, dp, seq):
        self.dp, self.seq, self.count = dp, seq, dp * seq
        self.plane = [1 << b for b in range(1, seq.bit_length() - 1)]
        self.depth = [seq << b for b in range(dp.bit_length() - 1)]

    def send(self, value, target):
        return lax.ppermute(value, AXES, [(i, target(i)) for i in range(self.count)])

    def flip(self, value, mask):
        return self.send(value, lambda i: i ^ mask)

    def order(self, index):
        return self.plane if index % 2 == 0 else self.plane[::-1]

    def level(self, value, level):
        return self.send(value, lambda i: i ^ self.order(i)[level])

    def slot_masks(self, index):
        half = self.seq // 2

        def mask(i, slot):
            return functools.reduce(
                lambda a, b: a ^ b,
                [m for level, m in enumerate(self.order(i)) if slot >> level & 1],
                0,
            )

        return [mask(index, s) for s in range(half)] + [1 ^ mask(index ^ 1, s) for s in range(half)]

    def seq_gather(self, value):
        pieces = [value]
        for slot in range(1, self.seq // 2):
            level = slot.bit_length() - 1
            pieces.append(self.level(pieces[slot ^ (1 << level)], level))
        return pieces + [self.flip(piece, 1) for piece in pieces]

    def seq_scatter(self, parts):
        half = self.seq // 2
        terms = [[parts[s], self.flip(parts[s + half], 1)] for s in range(half)]
        for slot in range(half - 1, 0, -1):
            level = slot.bit_length() - 1
            terms[slot ^ (1 << level)].append(self.level(total(terms[slot]).astype(BF16), level))
        return total(terms[0])

    def tree(self, bits):
        groups = {bit: bit if bit in self.plane else 0 for bit in bits}
        load = {group: 0 for group in groups.values()}
        far = [bit for bit in bits if bit in self.depth[1:]]
        parent = {}
        slots = sorted(
            (sum(bit for k, bit in enumerate(bits) if pick >> k & 1) for pick in range(1, 1 << len(bits))),
            key=lambda slot: (bin(slot).count("1"), slot),
        )

        def choices(slot):
            inside = [bit for bit in bits if slot & bit]
            near = [bit for bit in inside if bit not in far]
            return near or [max(inside)]

        for slot in sorted(slots, key=lambda slot: (len({groups[b] for b in choices(slot)}), slot)):
            bit = min(choices(slot), key=lambda b: (load[groups[b]], -b))
            load[groups[bit]] += 1
            parent[slot] = bit
        return [(slot, parent[slot]) for slot in slots]

    def gather(self, value, tree):
        pieces = {0: value}
        for slot, bit in tree:
            pieces[slot] = self.flip(pieces[slot ^ bit], bit)
        return [pieces[slot] for slot in [0] + [s for s, _ in tree]]

    def scatter(self, parts, tree):
        terms = {slot: [part] for slot, part in zip([0] + [s for s, _ in tree], parts)}
        for slot, bit in reversed(tree):
            terms[slot ^ bit].append(self.flip(total(terms[slot]).astype(BF16), bit))
        return total(terms[0])


def total(terms):
    result = terms[0].astype(F32)
    for term in terms[1:]:
        result = result + term.astype(F32)
    return result


def attend_kernel(q_ref, k_ref, v_ref, place_ref, start_ref, key_place_ref, o_ref, lse_ref):
    heads = q_ref.shape[0]
    keys, values = k_ref[...], v_ref[...]
    key_place = key_place_ref[...]
    allowed = (key_place <= place_ref[...]) & (key_place >= start_ref[...])
    for head in range(heads):
        scores = nt(q_ref[head], keys) * HEAD_DIM ** (-0.5)
        scores = jnp.where(allowed, scores, NEGATIVE)
        top = jnp.max(scores, axis=-1, keepdims=True)
        weights = jnp.exp(scores - top)
        whole = jnp.sum(weights, axis=-1, keepdims=True)
        out = nn(weights.astype(BF16), values) / whole
        o_ref[:, head * HEAD_DIM : (head + 1) * HEAD_DIM] = out.astype(BF16)
        lse_ref[:, head : head + 1] = top + jnp.log(whole)


def attend_back_kernel(
    q_ref, k_ref, v_ref, do_ref, lse_ref, place_ref, start_ref, key_place_ref, dq_ref, dk_ref, dv_ref
):
    heads = q_ref.shape[0]
    scale = HEAD_DIM ** (-0.5)

    @pl.when(pl.program_id(0) == 0)
    def _():
        dk_ref[...] = jnp.zeros_like(dk_ref)
        dv_ref[...] = jnp.zeros_like(dv_ref)

    keys, values = k_ref[...], v_ref[...]
    key_place = key_place_ref[...]
    allowed = (key_place <= place_ref[...]) & (key_place >= start_ref[...])
    for head in range(heads):
        query = q_ref[head]
        slope = do_ref[:, head * HEAD_DIM : (head + 1) * HEAD_DIM]
        scores = jnp.where(allowed, nt(query, keys) * scale, NEGATIVE)
        chance = jnp.exp(scores - lse_ref[:, head : head + 1])
        slope_chance = nt(slope, values)
        moved = chance * slope_chance
        offset = jnp.sum(moved, axis=-1, keepdims=True)
        slope_scores = (moved - chance * offset).astype(BF16)
        dq_ref[head] = nn(slope_scores, keys) * scale
        dk_ref[...] += tn(slope_scores, query) * scale
        dv_ref[...] += tn(chance.astype(BF16), slope)


def attend(query, keys, values, place, start, block):
    heads, length, width = query.shape
    rows = pl.BlockSpec((block, 1), lambda i: (i, 0))
    whole = pl.BlockSpec((length, width), lambda i: (0, 0))
    return pl.pallas_call(
        attend_kernel,
        grid=(length // block,),
        in_specs=[
            pl.BlockSpec((heads, block, width), lambda i: (0, i, 0)),
            whole,
            whole,
            rows,
            rows,
            pl.BlockSpec((1, length), lambda i: (0, 0)),
        ],
        out_specs=[
            pl.BlockSpec((block, heads * width), lambda i: (i, 0)),
            pl.BlockSpec((block, heads), lambda i: (i, 0)),
        ],
        out_shape=[
            jax.ShapeDtypeStruct((length, heads * width), BF16),
            jax.ShapeDtypeStruct((length, heads), F32),
        ],
        cost_estimate=pl.CostEstimate(
            flops=4 * heads * length * length * 256,
            transcendentals=heads * length * length,
            bytes_accessed=8 * heads * length * width,
        ),
        name="attend",
    )(query, keys, values, place[:, None], start[:, None], place[None, :])


def attend_back(query, keys, values, slope, lse, place, start, block):
    heads, length, width = query.shape
    rows = pl.BlockSpec((block, 1), lambda i: (i, 0))
    whole = pl.BlockSpec((length, width), lambda i: (0, 0))
    byhead = pl.BlockSpec((heads, block, width), lambda i: (0, i, 0))
    return pl.pallas_call(
        attend_back_kernel,
        grid=(length // block,),
        in_specs=[
            byhead,
            whole,
            whole,
            pl.BlockSpec((block, heads * width), lambda i: (i, 0)),
            pl.BlockSpec((block, heads), lambda i: (i, 0)),
            rows,
            rows,
            pl.BlockSpec((1, length), lambda i: (0, 0)),
        ],
        out_specs=[byhead, whole, whole],
        out_shape=[
            jax.ShapeDtypeStruct((heads, length, width), F32),
            jax.ShapeDtypeStruct((length, width), F32),
            jax.ShapeDtypeStruct((length, width), F32),
        ],
        cost_estimate=pl.CostEstimate(
            flops=10 * heads * length * length * 256,
            transcendentals=heads * length * length,
            bytes_accessed=16 * heads * length * width,
        ),
        name="attend_back",
    )(query, keys, values, slope, lse, place[:, None], start[:, None], place[None, :])


def split(value, count):
    size = value.shape[0] // count
    return [value[i * size : (i + 1) * size] for i in range(count)]


def feed(normed, slope, gate_up, down):
    both = nt(normed, gate_up)
    hidden_count = down.shape[0]
    gate, up = both[:, :hidden_count], both[:, hidden_count:]
    slope_hidden = nt(slope, down)
    bend = jax.nn.sigmoid(gate)
    curve = gate * bend
    hidden = (curve * up).astype(BF16)
    slope_gate = (slope_hidden * up * (bend * (1.0 + gate * (1.0 - bend)))).astype(BF16)
    slope_up = (slope_hidden * curve).astype(BF16)
    slope_both = jnp.concatenate([slope_gate, slope_up], axis=1)
    return hidden, slope_both


def on_device(
    layer_input,
    document_lengths,
    attention_gain,
    attention_in,
    query_gain,
    key_gain,
    attention_out,
    feed_gain,
    feed_weight,
    cotangent,
):
    dp, seq = lax.axis_size("dp"), lax.axis_size("seq")
    links = Links(dp, seq)
    count = links.count
    batch, length = layer_input.shape[0], layer_input.shape[1]
    tokens = batch * length
    here_dp, here = lax.axis_index("dp"), lax.axis_index("seq")
    q_heads = HEADS // seq
    shared = seq // KV_HEADS
    width = KV_HEADS * HEAD_DIM
    rows = attention_in.shape[0]

    masks = jnp.asarray(np.array([links.slot_masks(0), links.slot_masks(1)], np.int32))
    slot_seq = here ^ jnp.where(here % 2 == 0, masks[0], masks[1])
    place = (slot_seq[:, None] * length + jnp.arange(length)[None, :]).reshape(-1)
    lengths = document_lengths[0]
    ends = jnp.cumsum(lengths)
    start = jnp.sum(jnp.where(place[:, None] >= ends[None, :], lengths[None, :], 0), axis=1)
    half = HEAD_DIM // 2
    frequency = jnp.exp(jnp.arange(half).astype(F32) * (-2.0 * math.log(10000.0) / HEAD_DIM))
    angles = (place - start).astype(F32)[:, None] * frequency
    cosine, sine = jnp.cos(angles), jnp.sin(angles)

    w_query = attention_in[:, :D].reshape(rows, seq, q_heads * HEAD_DIM)
    w_key = attention_in[:, D : D + width].reshape(rows, KV_HEADS, HEAD_DIM)
    w_value = attention_in[:, D + width :].reshape(rows, KV_HEADS, HEAD_DIM)
    w_mine = jnp.concatenate(
        [w_query, jnp.repeat(w_key, shared, axis=1), jnp.repeat(w_value, shared, axis=1)], axis=2
    )
    w_mine = jnp.transpose(w_mine, (1, 0, 2))
    columns = w_mine.shape[2]
    w_in = lax.all_to_all(
        jnp.broadcast_to(w_mine[None], (dp,) + w_mine.shape).reshape(count, rows, columns),
        AXES, 0, 0, tiled=True,
    ).reshape(D, columns)

    w_slots = [
        links.send(attention_out, lambda i, m=m: ((i % dp + m) % dp) * seq + i // dp)
        for m in range(dp)
    ]
    w_out = jnp.concatenate(w_slots[::-1] + w_slots[::-1], axis=0)
    out_rows = dp * rows
    w_out = lax.dynamic_slice_in_dim(w_out, ((dp - 1 - here_dp) % dp) * rows, out_rows, 0)

    inputs = layer_input.astype(F32).reshape(tokens, D)
    normed = normalize(inputs, attention_gain).astype(BF16)
    normed_all = jnp.concatenate(links.seq_gather(normed), axis=0)
    joined = nn(normed_all, w_in)
    whole = normed_all.shape[0]

    def prepare(joined, query_gain, key_gain):
        split_key = q_heads * HEAD_DIM
        query = joined[:, :split_key].reshape(whole, q_heads, HEAD_DIM)
        keys = joined[:, split_key : split_key + HEAD_DIM]
        values = joined[:, split_key + HEAD_DIM :]
        query = rotate(normalize(query, query_gain), cosine[:, None], sine[:, None])
        keys = rotate(normalize(keys, key_gain), cosine, sine)
        return jnp.transpose(query, (1, 0, 2)), keys, values

    query, keys, values = prepare(joined, query_gain, key_gain)
    query, keys, values = query.astype(BF16), keys.astype(BF16), values.astype(BF16)
    attended, lse = attend(query, keys, values, place, start, length)
    branch = links.seq_scatter(split(nn(attended, w_out).astype(BF16), seq))
    resid = inputs + branch
    normed_feed = normalize(resid, feed_gain).astype(BF16)

    tree = links.tree(links.plane + links.depth)
    other = links.flip(feed_weight, 1)
    gate_up = jnp.concatenate(
        [feed_weight[:, :D], other[:, :D], feed_weight[:, D : 2 * D], other[:, D : 2 * D]], axis=0
    )
    down = jnp.concatenate([feed_weight[:, 2 * D :], other[:, 2 * D :]], axis=0)
    slope_out = cotangent.reshape(tokens, D)
    slots = len(tree) + 1
    chunked = []
    for low, slope in zip(split(normed_feed, CHUNKS), split(slope_out, CHUNKS)):
        low_all = jnp.concatenate(links.gather(low, tree), axis=0)
        slope_all = jnp.concatenate(links.gather(slope, tree), axis=0)
        hidden, slope_both = feed(low_all, slope_all, gate_up, down)
        chunked.append((low_all, slope_all, hidden, slope_both))
    slope_normed = jnp.concatenate(
        [
            links.scatter(split(nn(slope_both, gate_up).astype(BF16), slots), tree)
            for _, _, _, slope_both in chunked
        ],
        axis=0,
    )
    unused, norm_pull = jax.vjp(normalize, resid, feed_gain)
    slope_resid, feed_gain_part = norm_pull(slope_normed)
    slope_resid = slope_resid + slope_out.astype(F32)
    slope_branch = slope_resid.astype(BF16)

    mixed = jnp.concatenate(
        [
            links.scatter(split(nn(hidden, down).astype(BF16), slots), tree)
            for _, _, hidden, _ in chunked
        ],
        axis=0,
    )
    layer_output = (resid + mixed).astype(BF16).reshape(batch, length, D)

    low_all, slope_all, hidden, slope_both = [
        jnp.concatenate([chunk[k] for chunk in chunked], axis=0) for k in range(4)
    ]
    grad_both = tn(slope_both, low_all)
    grad_down = tn(hidden, slope_all)
    units = feed_weight.shape[0]
    mine = jnp.concatenate(
        [grad_both[:units], grad_both[2 * units : 3 * units], grad_down[:units]], axis=1
    )
    theirs = jnp.concatenate(
        [grad_both[units : 2 * units], grad_both[3 * units :], grad_down[units:]], axis=1
    )
    feed_weight_gradient = mine + links.flip(theirs.astype(BF16), 1).astype(F32)

    slope_branch_all = jnp.concatenate(links.seq_gather(slope_branch), axis=0)
    slope_low = nt(slope_branch_all, w_out).astype(BF16)
    grad_out = tn(attended, slope_branch_all).astype(BF16)
    grad_out = jnp.concatenate([grad_out, grad_out], axis=0)
    grad_out = lax.dynamic_slice_in_dim(grad_out, ((here_dp + 1) % dp) * rows, out_rows, 0)
    blocks = split(grad_out, dp)[::-1]
    pieces = []
    for m in range(dp):
        pairs = {((i % dp + m) % dp) * seq + i // dp: i for i in range(count)}
        pieces.append(links.send(blocks[m], lambda i, pairs=pairs: pairs[i]))
    attention_out_gradient = total(pieces)

    dq, dk, dv = attend_back(query, keys, values, slope_low, lse, place, start, length)
    unused, prepare_pull = jax.vjp(prepare, joined, query_gain, key_gain)
    slope_joined, query_gain_part, key_gain_part = prepare_pull((dq, dk, dv))
    slope_joined = slope_joined.astype(BF16)
    slope_first = links.seq_scatter(split(nt(slope_joined, w_in).astype(BF16), seq))
    grad_in = tn(normed_all, slope_joined).astype(BF16).reshape(count, rows, columns)
    grad_in = lax.all_to_all(grad_in, AXES, 0, 0, tiled=True).astype(F32)
    grad_in = jnp.sum(grad_in.reshape(dp, seq, rows, columns), axis=0)
    split_key = q_heads * HEAD_DIM
    grad_query = jnp.transpose(grad_in[:, :, :split_key], (1, 0, 2)).reshape(rows, D)
    grad_key = jnp.sum(
        grad_in[:, :, split_key : split_key + HEAD_DIM].reshape(KV_HEADS, shared, rows, HEAD_DIM), axis=1
    )
    grad_value = jnp.sum(
        grad_in[:, :, split_key + HEAD_DIM :].reshape(KV_HEADS, shared, rows, HEAD_DIM), axis=1
    )
    attention_in_gradient = jnp.concatenate(
        [
            grad_query,
            jnp.transpose(grad_key, (1, 0, 2)).reshape(rows, width),
            jnp.transpose(grad_value, (1, 0, 2)).reshape(rows, width),
        ],
        axis=1,
    )
    unused, first_pull = jax.vjp(normalize, inputs, attention_gain)
    slope_inputs, attention_gain_part = first_pull(slope_first)
    input_gradient = (slope_resid + slope_inputs).astype(BF16).reshape(batch, length, D)
    gains = lax.psum(
        jnp.concatenate([attention_gain_part, query_gain_part, key_gain_part, feed_gain_part]), AXES
    )
    cut = [D, D + HEAD_DIM, D + 2 * HEAD_DIM]
    return (
        layer_output,
        input_gradient,
        gains[: cut[0]],
        attention_in_gradient,
        gains[cut[0] : cut[1]],
        gains[cut[1] : cut[2]],
        attention_out_gradient,
        gains[cut[2] :],
        feed_weight_gradient,
    )


def solution(mesh):
    tokens = P("dp", "seq", None)
    rows = P(("dp", "seq"), None)
    return jax.shard_map(
        on_device,
        mesh=mesh,
        in_specs=(tokens, P("dp", None), P(), rows, P(), P(), rows, P(), rows, tokens),
        out_specs=(tokens, tokens, P(), rows, P(), P(), rows, P(), rows),
        check_vma=False,
    )
```

```python
import functools
import math

import jax
import jax.numpy as jnp
import numpy as np
from jax import lax
from jax.experimental import pallas as pl
from jax.experimental.pallas import tpu as pltpu
from jax.sharding import PartitionSpec as P

D = 2048
HEADS = 32
KV_HEADS = 8
HEAD_DIM = 64
EPSILON = 1e-06
NEGATIVE = -1e30
AXES = ("dp", "seq")
F32 = jnp.float32
BF16 = jnp.bfloat16


def nt(left, right):
    return lax.dot_general(left, right, (((1,), (1,)), ((), ())), preferred_element_type=F32)


def nn(left, right):
    return jnp.dot(left, right, preferred_element_type=F32)


def tn(left, right):
    return lax.dot_general(left, right, (((0,), (0,)), ((), ())), preferred_element_type=F32)


def normalize(value, gain):
    return value * lax.rsqrt(jnp.mean(value * value, axis=-1, keepdims=True) + EPSILON) * gain


def rotate(value, cosine, sine):
    half = value.shape[-1] // 2
    first = value[..., :half]
    second = value[..., half:]
    return jnp.concatenate(
        [first * cosine - second * sine, second * cosine + first * sine], axis=-1
    )


class Links:
    def __init__(self, dp, seq):
        self.dp, self.seq, self.count = dp, seq, dp * seq
        plane = [1 << b for b in range(1, seq.bit_length() - 1)]
        depth = [seq << b for b in range(dp.bit_length() - 1)]
        both = lambda bits: [(bit, bit) for bit in bits]
        self.core = both([1])
        self.plane = list(zip(plane, plane[::-1]))
        self.near = both(depth[:1])
        self.sequence = self.plane + self.core
        self.tokens = both(depth[1:][::-1]) + self.plane
        self.every = both([1] + plane + depth)

    def send(self, value, target):
        return lax.ppermute(value, AXES, [(i, target(i)) for i in range(self.count)])

    def flip(self, value, level):
        return self.send(value, lambda i: i ^ level[i % 2])

    def slot_masks(self, index):
        masks = [0]
        for level in self.plane:
            masks = masks + [mask ^ level[index % 2] for mask in masks]
        other = [0]
        for level in self.plane:
            other = other + [mask ^ level[(index + 1) % 2] for mask in other]
        return masks + [mask ^ 1 for mask in other]

    def gather(self, value, levels):
        for level in levels:
            value = jnp.concatenate([value, self.flip(value, level)], axis=0)
        return value

    def scatter(self, kept, sent, levels):
        for level in levels[::-1]:
            got = self.flip(sent, level)
            half = kept.shape[0] // 2
            if level is levels[0]:
                return kept.astype(F32) + got.astype(F32)
            sent = (kept[half:].astype(F32) + got[half:].astype(F32)).astype(BF16)
            kept = kept[:half].astype(F32) + got[:half].astype(F32)


def attend_kernel(q_ref, k_ref, v_ref, place_ref, start_ref, key_place_ref, o_ref, lse_ref):
    heads = q_ref.shape[0]
    keys, values = k_ref[...], v_ref[...]
    key_place = key_place_ref[...]
    allowed = (key_place <= place_ref[...]) & (key_place >= start_ref[...])
    for head in range(heads):
        scores = nt(q_ref[head], keys) * HEAD_DIM ** (-0.5)
        scores = jnp.where(allowed, scores, NEGATIVE)
        top = jnp.max(scores, axis=-1, keepdims=True)
        weights = jnp.exp(scores - top)
        whole = jnp.sum(weights, axis=-1, keepdims=True)
        out = nn(weights.astype(BF16), values) / whole
        o_ref[:, head * HEAD_DIM : (head + 1) * HEAD_DIM] = out.astype(BF16)
        lse_ref[:, head : head + 1] = top + jnp.log(whole)


def attend_back_kernel(
    q_ref, k_ref, v_ref, do_ref, lse_ref, place_ref, start_ref, key_place_ref, dq_ref, dk_ref, dv_ref
):
    heads = q_ref.shape[0]
    scale = HEAD_DIM ** (-0.5)

    @pl.when(pl.program_id(0) == 0)
    def _():
        dk_ref[...] = jnp.zeros_like(dk_ref)
        dv_ref[...] = jnp.zeros_like(dv_ref)

    keys, values = k_ref[...], v_ref[...]
    key_place = key_place_ref[...]
    allowed = (key_place <= place_ref[...]) & (key_place >= start_ref[...])
    for head in range(heads):
        query = q_ref[head]
        slope = do_ref[:, head * HEAD_DIM : (head + 1) * HEAD_DIM]
        scores = jnp.where(allowed, nt(query, keys) * scale, NEGATIVE)
        chance = jnp.exp(scores - lse_ref[:, head : head + 1])
        slope_chance = nt(slope, values)
        moved = chance * slope_chance
        offset = jnp.sum(moved, axis=-1, keepdims=True)
        slope_scores = (moved - chance * offset).astype(BF16)
        dq_ref[head] = nn(slope_scores, keys) * scale
        dk_ref[...] += tn(slope_scores, query) * scale
        dv_ref[...] += tn(chance.astype(BF16), slope)


def attend(query, keys, values, place, start, block):
    heads, length, width = query.shape
    rows = pl.BlockSpec((block, 1), lambda i: (i, 0))
    whole = pl.BlockSpec((length, width), lambda i: (0, 0))
    return pl.pallas_call(
        attend_kernel,
        grid=(length // block,),
        in_specs=[
            pl.BlockSpec((heads, block, width), lambda i: (0, i, 0)),
            whole,
            whole,
            rows,
            rows,
            pl.BlockSpec((1, length), lambda i: (0, 0)),
        ],
        out_specs=[
            pl.BlockSpec((block, heads * width), lambda i: (i, 0)),
            pl.BlockSpec((block, heads), lambda i: (i, 0)),
        ],
        out_shape=[
            jax.ShapeDtypeStruct((length, heads * width), BF16),
            jax.ShapeDtypeStruct((length, heads), F32),
        ],
        cost_estimate=pl.CostEstimate(
            flops=4 * heads * length * length * 256,
            transcendentals=heads * length * length,
            bytes_accessed=8 * heads * length * width,
        ),
        name="attend",
    )(query, keys, values, place[:, None], start[:, None], place[None, :])


def attend_back(query, keys, values, slope, lse, place, start, block):
    heads, length, width = query.shape
    rows = pl.BlockSpec((block, 1), lambda i: (i, 0))
    whole = pl.BlockSpec((length, width), lambda i: (0, 0))
    byhead = pl.BlockSpec((heads, block, width), lambda i: (0, i, 0))
    return pl.pallas_call(
        attend_back_kernel,
        grid=(length // block,),
        in_specs=[
            byhead,
            whole,
            whole,
            pl.BlockSpec((block, heads * width), lambda i: (i, 0)),
            pl.BlockSpec((block, heads), lambda i: (i, 0)),
            rows,
            rows,
            pl.BlockSpec((1, length), lambda i: (0, 0)),
        ],
        out_specs=[byhead, whole, whole],
        out_shape=[
            jax.ShapeDtypeStruct((heads, length, width), F32),
            jax.ShapeDtypeStruct((length, width), F32),
            jax.ShapeDtypeStruct((length, width), F32),
        ],
        cost_estimate=pl.CostEstimate(
            flops=10 * heads * length * length * 256,
            transcendentals=heads * length * length,
            bytes_accessed=16 * heads * length * width,
        ),
        name="attend_back",
    )(query, keys, values, slope, lse, place[:, None], start[:, None], place[None, :])


def split(value, count):
    size = value.shape[0] // count
    return [value[i * size : (i + 1) * size] for i in range(count)]


def feed(normed, slope, gate_up, down):
    both = nt(normed, gate_up)
    hidden_count = down.shape[0]
    gate, up = both[:, :hidden_count], both[:, hidden_count:]
    slope_hidden = nt(slope, down)
    bend = jax.nn.sigmoid(gate)
    curve = gate * bend
    hidden = (curve * up).astype(BF16)
    slope_gate = (slope_hidden * up * (bend * (1.0 + gate * (1.0 - bend)))).astype(BF16)
    slope_up = (slope_hidden * curve).astype(BF16)
    slope_both = jnp.concatenate([slope_gate, slope_up], axis=1)
    return hidden, slope_both


def on_device(
    layer_input,
    document_lengths,
    attention_gain,
    attention_in,
    query_gain,
    key_gain,
    attention_out,
    feed_gain,
    feed_weight,
    cotangent,
):
    dp, seq = lax.axis_size("dp"), lax.axis_size("seq")
    links = Links(dp, seq)
    count = links.count
    batch, length = layer_input.shape[0], layer_input.shape[1]
    tokens = batch * length
    here_dp, here = lax.axis_index("dp"), lax.axis_index("seq")
    q_heads = HEADS // seq
    shared = seq // KV_HEADS
    width = KV_HEADS * HEAD_DIM
    rows = attention_in.shape[0]

    masks = jnp.asarray(np.array([links.slot_masks(0), links.slot_masks(1)], np.int32))
    slot_seq = here ^ jnp.where(here % 2 == 0, masks[0], masks[1])
    place = (slot_seq[:, None] * length + jnp.arange(length)[None, :]).reshape(-1)
    lengths = document_lengths[0]
    ends = jnp.cumsum(lengths)
    start = jnp.sum(jnp.where(place[:, None] >= ends[None, :], lengths[None, :], 0), axis=1)
    half = HEAD_DIM // 2
    frequency = jnp.exp(jnp.arange(half).astype(F32) * (-2.0 * math.log(10000.0) / HEAD_DIM))
    angles = (place - start).astype(F32)[:, None] * frequency
    cosine, sine = jnp.cos(angles), jnp.sin(angles)

    w_query = attention_in[:, :D].reshape(rows, seq, q_heads * HEAD_DIM)
    w_key = attention_in[:, D : D + width].reshape(rows, KV_HEADS, HEAD_DIM)
    w_value = attention_in[:, D + width :].reshape(rows, KV_HEADS, HEAD_DIM)
    w_mine = jnp.concatenate(
        [w_query, jnp.repeat(w_key, shared, axis=1), jnp.repeat(w_value, shared, axis=1)], axis=2
    )
    w_mine = jnp.transpose(w_mine, (1, 0, 2))
    columns = w_mine.shape[2]
    w_in = lax.all_to_all(
        jnp.broadcast_to(w_mine[None], (dp,) + w_mine.shape).reshape(count, rows, columns),
        AXES, 0, 0, tiled=True,
    ).reshape(D, columns)

    w_slots = [
        links.send(attention_out, lambda i, m=m: ((i % dp + m) % dp) * seq + i // dp)
        for m in range(dp)
    ]
    w_out = jnp.concatenate(w_slots[::-1] + w_slots[::-1], axis=0)
    out_rows = dp * rows
    w_out = lax.dynamic_slice_in_dim(w_out, ((dp - 1 - here_dp) % dp) * rows, out_rows, 0)

    inputs = layer_input.astype(F32).reshape(tokens, D)
    normed = normalize(inputs, attention_gain).astype(BF16)
    normed_all = links.gather(normed, links.sequence)
    joined = nn(normed_all, w_in)
    whole = normed_all.shape[0]

    def prepare(joined, query_gain, key_gain):
        split_key = q_heads * HEAD_DIM
        query = joined[:, :split_key].reshape(whole, q_heads, HEAD_DIM)
        keys = joined[:, split_key : split_key + HEAD_DIM]
        values = joined[:, split_key + HEAD_DIM :]
        query = rotate(normalize(query, query_gain), cosine[:, None], sine[:, None])
        keys = rotate(normalize(keys, key_gain), cosine, sine)
        return jnp.transpose(query, (1, 0, 2)), keys, values

    query, keys, values = prepare(joined, query_gain, key_gain)
    query, keys, values = query.astype(BF16), keys.astype(BF16), values.astype(BF16)
    attended, lse = attend(query, keys, values, place, start, length)
    middle = whole // 2
    sent = nn(attended[middle:], w_out).astype(BF16)
    branch = links.scatter(nn(attended[:middle], w_out), sent, links.sequence)
    resid = inputs + branch
    normed_feed = normalize(resid, feed_gain).astype(BF16)

    near = links.flip(feed_weight, links.near[0])
    shares = [feed_weight, near, links.flip(feed_weight, links.core[0]), links.flip(near, links.core[0])]
    gate_up = jnp.concatenate(
        [share[:, :D] for share in shares] + [share[:, D : 2 * D] for share in shares], axis=0
    )
    down = jnp.concatenate([share[:, 2 * D :] for share in shares], axis=0)
    units = down.shape[0]
    slope_out = cotangent.reshape(tokens, D)
    first_levels, last_level = links.tokens[:-1], links.tokens[-1]
    slope_first_half = links.gather(slope_out, first_levels)
    slope_last_half = links.flip(slope_first_half, last_level)
    low_first = links.gather(normed_feed, first_levels)
    low_last = links.flip(low_first, last_level)
    hidden_first, both_first = feed(low_first, slope_first_half, gate_up, down)
    hidden_last, both_last = feed(low_last, slope_last_half, gate_up, down)
    sent = nn(both_last, gate_up).astype(BF16)
    slope_normed = links.scatter(nn(both_first, gate_up), sent, links.tokens)
    unused, norm_pull = jax.vjp(normalize, resid, feed_gain)
    slope_resid, feed_gain_part = norm_pull(slope_normed)
    slope_resid = slope_resid + slope_out.astype(F32)
    slope_branch = slope_resid.astype(BF16)

    grad_both = tn(both_first, low_first) + tn(both_last, low_last)
    grad_down = tn(hidden_first, slope_first_half) + tn(hidden_last, slope_last_half)
    parts = []
    for part in (grad_both[:units], grad_both[units:], grad_down):
        parts.append(
            links.scatter(part[: units // 2], part[units // 2 :].astype(BF16), links.near + links.core)
        )
    feed_weight_gradient = jnp.concatenate(parts, axis=1)

    hidden_first, hidden_last, slope_branch = lax.optimization_barrier(
        (hidden_first, hidden_last, slope_branch)
    )
    mixed = links.scatter(
        nn(hidden_first, down), nn(hidden_last, down).astype(BF16), links.tokens
    )
    layer_output = (resid + mixed).astype(BF16).reshape(batch, length, D)

    slope_branch_all = links.gather(slope_branch, links.sequence)
    slope_low = nt(slope_branch_all, w_out).astype(BF16)
    grad_out = tn(attended, slope_branch_all).astype(BF16)
    grad_out = jnp.concatenate([grad_out, grad_out], axis=0)
    grad_out = lax.dynamic_slice_in_dim(grad_out, ((here_dp + 1) % dp) * rows, out_rows, 0)
    blocks = split(grad_out, dp)[::-1]
    pieces = []
    for m in range(dp):
        pairs = {((i % dp + m) % dp) * seq + i // dp: i for i in range(count)}
        pieces.append(links.send(blocks[m], lambda i, pairs=pairs: pairs[i]))
    attention_out_gradient = sum(piece.astype(F32) for piece in pieces)

    dq, dk, dv = attend_back(query, keys, values, slope_low, lse, place, start, length)
    unused, prepare_pull = jax.vjp(prepare, joined, query_gain, key_gain)
    slope_joined, query_gain_part, key_gain_part = prepare_pull((dq, dk, dv))
    slope_joined = slope_joined.astype(BF16)
    grad_in = tn(normed_all, slope_joined)
    attention_gain_part = jnp.sum(grad_in * w_in.astype(F32), axis=1) / attention_gain
    grad_in = grad_in.astype(BF16).reshape(count, rows, columns)
    sent = nt(slope_joined[middle:], w_in).astype(BF16)
    slope_first = links.scatter(nt(slope_joined[:middle], w_in), sent, links.sequence)
    grad_in = lax.all_to_all(grad_in, AXES, 0, 0, tiled=True).astype(F32)
    grad_in = jnp.sum(grad_in.reshape(dp, seq, rows, columns), axis=0)
    split_key = q_heads * HEAD_DIM
    grad_query = jnp.transpose(grad_in[:, :, :split_key], (1, 0, 2)).reshape(rows, D)
    grad_key = jnp.sum(
        grad_in[:, :, split_key : split_key + HEAD_DIM].reshape(KV_HEADS, shared, rows, HEAD_DIM), axis=1
    )
    grad_value = jnp.sum(
        grad_in[:, :, split_key + HEAD_DIM :].reshape(KV_HEADS, shared, rows, HEAD_DIM), axis=1
    )
    attention_in_gradient = jnp.concatenate(
        [
            grad_query,
            jnp.transpose(grad_key, (1, 0, 2)).reshape(rows, width),
            jnp.transpose(grad_value, (1, 0, 2)).reshape(rows, width),
        ],
        axis=1,
    )
    unused, first_pull = jax.vjp(lambda v: normalize(v, attention_gain), inputs)
    (slope_inputs,) = first_pull(slope_first)
    input_gradient = (slope_resid + slope_inputs).astype(BF16).reshape(batch, length, D)
    gains = jnp.concatenate([attention_gain_part, query_gain_part, key_gain_part, feed_gain_part])
    gains = gains.reshape(-1, 2 * HEAD_DIM)
    for level in links.every:
        gains = gains + links.flip(gains, level)
    gains = gains.reshape(-1)
    cut = [D, D + HEAD_DIM, D + 2 * HEAD_DIM]
    return (
        layer_output,
        input_gradient,
        gains[: cut[0]],
        attention_in_gradient,
        gains[cut[0] : cut[1]],
        gains[cut[1] : cut[2]],
        attention_out_gradient,
        gains[cut[2] :],
        feed_weight_gradient,
    )


def solution(mesh):
    tokens = P("dp", "seq", None)
    rows = P(("dp", "seq"), None)
    return jax.shard_map(
        on_device,
        mesh=mesh,
        in_specs=(tokens, P("dp", None), P(), rows, P(), P(), rows, P(), rows, tokens),
        out_specs=(tokens, tokens, P(), rows, P(), P(), rows, P(), rows),
        check_vma=False,
    )
```

```python
import functools
import math

import jax
import jax.numpy as jnp
import numpy as np
from jax import lax
from jax.experimental import pallas as pl
from jax.experimental.pallas import tpu as pltpu
from jax.sharding import PartitionSpec as P

D = 2048
HEADS = 32
KV_HEADS = 8
HEAD_DIM = 64
EPSILON = 1e-06
NEGATIVE = -1e30
AXES = ("dp", "seq")
F32 = jnp.float32
BF16 = jnp.bfloat16


def nt(left, right):
    return lax.dot_general(left, right, (((1,), (1,)), ((), ())), preferred_element_type=F32)


def nn(left, right):
    return jnp.dot(left, right, preferred_element_type=F32)


def tn(left, right):
    return lax.dot_general(left, right, (((0,), (0,)), ((), ())), preferred_element_type=F32)


def normalize(value, gain):
    return value * lax.rsqrt(jnp.mean(value * value, axis=-1, keepdims=True) + EPSILON) * gain


def rotate(value, cosine, sine):
    half = value.shape[-1] // 2
    first = value[..., :half]
    second = value[..., half:]
    return jnp.concatenate(
        [first * cosine - second * sine, second * cosine + first * sine], axis=-1
    )


class Links:
    def __init__(self, dp, seq):
        self.dp, self.seq, self.count = dp, seq, dp * seq
        plane = [1 << b for b in range(1, seq.bit_length() - 1)]
        depth = [seq << b for b in range(dp.bit_length() - 1)]
        both = lambda bits: [(bit, bit) for bit in bits]
        self.core = both([1])
        self.plane = list(zip(plane, plane[::-1]))
        self.near = both(depth[:1])
        self.sequence = self.plane + self.core
        self.tokens = both(depth[1:][::-1]) + self.plane
        self.every = both([1] + depth + plane)

    def send(self, value, target):
        return lax.ppermute(value, AXES, [(i, target(i)) for i in range(self.count)])

    def flip(self, value, level):
        return self.send(value, lambda i: i ^ level[i % 2])

    def slot_masks(self, index):
        masks = [0]
        for level in self.plane:
            masks = masks + [mask ^ level[index % 2] for mask in masks]
        other = [0]
        for level in self.plane:
            other = other + [mask ^ level[(index + 1) % 2] for mask in other]
        return masks + [mask ^ 1 for mask in other]

    def gather(self, value, levels):
        for level in levels:
            value = jnp.concatenate([value, self.flip(value, level)], axis=0)
        return value

    def scatter(self, kept, sent, levels):
        for level in levels[::-1]:
            got = self.flip(sent, level)
            half = kept.shape[0] // 2
            if level is levels[0]:
                return kept.astype(F32) + got.astype(F32)
            sent = (kept[half:].astype(F32) + got[half:].astype(F32)).astype(BF16)
            kept = kept[:half].astype(F32) + got[:half].astype(F32)

    def scatter_beside(self, kept, sent, levels, small, small_levels):
        ends = [1 + (len(small_levels) - 1) * i // (len(levels) - 1) for i in range(len(levels))]
        done = 0
        for level, end in zip(levels[::-1], ends):
            got = self.flip(sent, level)
            for small_level in small_levels[done:end]:
                small = small + self.flip(small, small_level)
            done = end
            half = kept.shape[0] // 2
            if level is levels[0]:
                return kept.astype(F32) + got.astype(F32), small
            sent = (kept[half:].astype(F32) + got[half:].astype(F32)).astype(BF16)
            kept = kept[:half].astype(F32) + got[:half].astype(F32)
            sent, small = lax.optimization_barrier((sent, small))


def attend_kernel(q_ref, k_ref, v_ref, place_ref, start_ref, key_place_ref, o_ref, lse_ref):
    heads = q_ref.shape[0]
    keys, values = k_ref[...], v_ref[...]
    key_place = key_place_ref[...]
    allowed = (key_place <= place_ref[...]) & (key_place >= start_ref[...])
    for head in range(heads):
        scores = nt(q_ref[head], keys) * HEAD_DIM ** (-0.5)
        scores = jnp.where(allowed, scores, NEGATIVE)
        top = jnp.max(scores, axis=-1, keepdims=True)
        weights = jnp.exp(scores - top)
        whole = jnp.sum(weights, axis=-1, keepdims=True)
        out = nn(weights.astype(BF16), values) / whole
        o_ref[:, head * HEAD_DIM : (head + 1) * HEAD_DIM] = out.astype(BF16)
        lse_ref[:, head : head + 1] = top + jnp.log(whole)


def attend_back_kernel(
    q_ref, k_ref, v_ref, do_ref, lse_ref, place_ref, start_ref, key_place_ref, dq_ref, dk_ref, dv_ref
):
    heads = q_ref.shape[0]
    scale = HEAD_DIM ** (-0.5)

    @pl.when(pl.program_id(0) == 0)
    def _():
        dk_ref[...] = jnp.zeros_like(dk_ref)
        dv_ref[...] = jnp.zeros_like(dv_ref)

    keys, values = k_ref[...], v_ref[...]
    key_place = key_place_ref[...]
    allowed = (key_place <= place_ref[...]) & (key_place >= start_ref[...])
    for head in range(heads):
        query = q_ref[head]
        slope = do_ref[:, head * HEAD_DIM : (head + 1) * HEAD_DIM]
        scores = jnp.where(allowed, nt(query, keys) * scale, NEGATIVE)
        chance = jnp.exp(scores - lse_ref[:, head : head + 1])
        slope_chance = nt(slope, values)
        moved = chance * slope_chance
        offset = jnp.sum(moved, axis=-1, keepdims=True)
        slope_scores = (moved - chance * offset).astype(BF16)
        dq_ref[head] = nn(slope_scores, keys) * scale
        dk_ref[...] += tn(slope_scores, query) * scale
        dv_ref[...] += tn(chance.astype(BF16), slope)


def attend(query, keys, values, place, start, block):
    heads, length, width = query.shape
    rows = pl.BlockSpec((block, 1), lambda i: (i, 0))
    whole = pl.BlockSpec((length, width), lambda i: (0, 0))
    return pl.pallas_call(
        attend_kernel,
        grid=(length // block,),
        in_specs=[
            pl.BlockSpec((heads, block, width), lambda i: (0, i, 0)),
            whole,
            whole,
            rows,
            rows,
            pl.BlockSpec((1, length), lambda i: (0, 0)),
        ],
        out_specs=[
            pl.BlockSpec((block, heads * width), lambda i: (i, 0)),
            pl.BlockSpec((block, heads), lambda i: (i, 0)),
        ],
        out_shape=[
            jax.ShapeDtypeStruct((length, heads * width), BF16),
            jax.ShapeDtypeStruct((length, heads), F32),
        ],
        cost_estimate=pl.CostEstimate(
            flops=4 * heads * length * length * 256,
            transcendentals=heads * length * length,
            bytes_accessed=8 * heads * length * width,
        ),
        name="attend",
    )(query, keys, values, place[:, None], start[:, None], place[None, :])


def attend_back(query, keys, values, slope, lse, place, start, block):
    heads, length, width = query.shape
    rows = pl.BlockSpec((block, 1), lambda i: (i, 0))
    whole = pl.BlockSpec((length, width), lambda i: (0, 0))
    byhead = pl.BlockSpec((heads, block, width), lambda i: (0, i, 0))
    return pl.pallas_call(
        attend_back_kernel,
        grid=(length // block,),
        in_specs=[
            byhead,
            whole,
            whole,
            pl.BlockSpec((block, heads * width), lambda i: (i, 0)),
            pl.BlockSpec((block, heads), lambda i: (i, 0)),
            rows,
            rows,
            pl.BlockSpec((1, length), lambda i: (0, 0)),
        ],
        out_specs=[byhead, whole, whole],
        out_shape=[
            jax.ShapeDtypeStruct((heads, length, width), F32),
            jax.ShapeDtypeStruct((length, width), F32),
            jax.ShapeDtypeStruct((length, width), F32),
        ],
        cost_estimate=pl.CostEstimate(
            flops=10 * heads * length * length * 256,
            transcendentals=heads * length * length,
            bytes_accessed=16 * heads * length * width,
        ),
        name="attend_back",
    )(query, keys, values, slope, lse, place[:, None], start[:, None], place[None, :])


def split(value, count):
    size = value.shape[0] // count
    return [value[i * size : (i + 1) * size] for i in range(count)]


def feed(normed, slope, gate_up, down):
    both = nt(normed, gate_up)
    hidden_count = down.shape[0]
    gate, up = both[:, :hidden_count], both[:, hidden_count:]
    slope_hidden = nt(slope, down)
    bend = jax.nn.sigmoid(gate)
    curve = gate * bend
    hidden = (curve * up).astype(BF16)
    slope_gate = (slope_hidden * up * (bend * (1.0 + gate * (1.0 - bend)))).astype(BF16)
    slope_up = (slope_hidden * curve).astype(BF16)
    slope_both = jnp.concatenate([slope_gate, slope_up], axis=1)
    return hidden, slope_both


def on_device(
    layer_input,
    document_lengths,
    attention_gain,
    attention_in,
    query_gain,
    key_gain,
    attention_out,
    feed_gain,
    feed_weight,
    cotangent,
):
    dp, seq = lax.axis_size("dp"), lax.axis_size("seq")
    links = Links(dp, seq)
    count = links.count
    batch, length = layer_input.shape[0], layer_input.shape[1]
    tokens = batch * length
    here_dp, here = lax.axis_index("dp"), lax.axis_index("seq")
    q_heads = HEADS // seq
    shared = seq // KV_HEADS
    width = KV_HEADS * HEAD_DIM
    rows = attention_in.shape[0]

    masks = jnp.asarray(np.array([links.slot_masks(0), links.slot_masks(1)], np.int32))
    slot_seq = here ^ jnp.where(here % 2 == 0, masks[0], masks[1])
    place = (slot_seq[:, None] * length + jnp.arange(length)[None, :]).reshape(-1)
    lengths = document_lengths[0]
    ends = jnp.cumsum(lengths)
    start = jnp.sum(jnp.where(place[:, None] >= ends[None, :], lengths[None, :], 0), axis=1)
    half = HEAD_DIM // 2
    frequency = jnp.exp(jnp.arange(half).astype(F32) * (-2.0 * math.log(10000.0) / HEAD_DIM))
    angles = (place - start).astype(F32)[:, None] * frequency
    cosine, sine = jnp.cos(angles), jnp.sin(angles)

    w_query = attention_in[:, :D].reshape(rows, seq, q_heads * HEAD_DIM)
    w_key = attention_in[:, D : D + width].reshape(rows, KV_HEADS, HEAD_DIM)
    w_value = attention_in[:, D + width :].reshape(rows, KV_HEADS, HEAD_DIM)
    w_mine = jnp.concatenate(
        [w_query, jnp.repeat(w_key, shared, axis=1), jnp.repeat(w_value, shared, axis=1)], axis=2
    )
    w_mine = jnp.transpose(w_mine, (1, 0, 2))
    columns = w_mine.shape[2]
    w_in = lax.all_to_all(
        jnp.broadcast_to(w_mine[None], (dp,) + w_mine.shape).reshape(count, rows, columns),
        AXES, 0, 0, tiled=True,
    ).reshape(D, columns)

    w_slots = [
        links.send(attention_out, lambda i, m=m: ((i % dp + m) % dp) * seq + i // dp)
        for m in range(dp)
    ]
    w_out = jnp.concatenate(w_slots[::-1] + w_slots[::-1], axis=0)
    out_rows = dp * rows
    w_out = lax.dynamic_slice_in_dim(w_out, ((dp - 1 - here_dp) % dp) * rows, out_rows, 0)

    inputs = layer_input.astype(F32).reshape(tokens, D)
    normed = normalize(inputs, attention_gain).astype(BF16)
    normed_all = links.gather(normed, links.sequence)
    joined = nn(normed_all, w_in)
    whole = normed_all.shape[0]

    def prepare(joined, query_gain, key_gain):
        split_key = q_heads * HEAD_DIM
        query = joined[:, :split_key].reshape(whole, q_heads, HEAD_DIM)
        keys = joined[:, split_key : split_key + HEAD_DIM]
        values = joined[:, split_key + HEAD_DIM :]
        query = rotate(normalize(query, query_gain), cosine[:, None], sine[:, None])
        keys = rotate(normalize(keys, key_gain), cosine, sine)
        return jnp.transpose(query, (1, 0, 2)), keys, values

    query, keys, values = prepare(joined, query_gain, key_gain)
    query, keys, values = query.astype(BF16), keys.astype(BF16), values.astype(BF16)
    slope_out = cotangent.reshape(tokens, D)
    first_levels, last_level = links.tokens[:-1], links.tokens[-1]
    slope_first_half = links.gather(slope_out, first_levels)
    query, keys, values, slope_first_half = lax.optimization_barrier(
        (query, keys, values, slope_first_half)
    )
    attended, lse = attend(query, keys, values, place, start, length)
    middle = whole // 2
    sent = nn(attended[middle:], w_out).astype(BF16)
    branch = links.scatter(nn(attended[:middle], w_out), sent, links.sequence)
    resid = inputs + branch
    normed_feed = normalize(resid, feed_gain).astype(BF16)

    near = links.flip(feed_weight, links.near[0])
    shares = [feed_weight, near, links.flip(feed_weight, links.core[0]), links.flip(near, links.core[0])]
    gate_up = jnp.concatenate(
        [share[:, :D] for share in shares] + [share[:, D : 2 * D] for share in shares], axis=0
    )
    down = jnp.concatenate([share[:, 2 * D :] for share in shares], axis=0)
    units = down.shape[0]
    slope_last_half = links.flip(slope_first_half, last_level)
    low_first = links.gather(normed_feed, first_levels)
    low_last = links.flip(low_first, last_level)
    hidden_first, both_first = feed(low_first, slope_first_half, gate_up, down)
    hidden_last, both_last = feed(low_last, slope_last_half, gate_up, down)
    sent = nn(both_last, gate_up).astype(BF16)
    slope_normed = links.scatter(nn(both_first, gate_up), sent, links.tokens)
    unused, norm_pull = jax.vjp(normalize, resid, feed_gain)
    slope_resid, feed_gain_part = norm_pull(slope_normed)
    slope_resid = slope_resid + slope_out.astype(F32)
    slope_branch = slope_resid.astype(BF16)

    grad_both = tn(both_first, low_first) + tn(both_last, low_last)
    grad_down = tn(hidden_first, slope_first_half) + tn(hidden_last, slope_last_half)
    parts = []
    for part in (grad_both[:units], grad_both[units:], grad_down):
        parts.append(
            links.scatter(part[: units // 2], part[units // 2 :].astype(BF16), links.near + links.core)
        )
    feed_weight_gradient = jnp.concatenate(parts, axis=1)

    hidden_first, hidden_last, slope_branch = lax.optimization_barrier(
        (hidden_first, hidden_last, slope_branch)
    )
    mixed = links.scatter(
        nn(hidden_first, down), nn(hidden_last, down).astype(BF16), links.tokens
    )
    layer_output = (resid + mixed).astype(BF16).reshape(batch, length, D)

    slope_branch_all = links.gather(slope_branch, links.sequence)
    slope_low = nt(slope_branch_all, w_out).astype(BF16)
    grad_out = tn(attended, slope_branch_all).astype(BF16)
    grad_out = jnp.concatenate([grad_out, grad_out], axis=0)
    grad_out = lax.dynamic_slice_in_dim(grad_out, ((here_dp + 1) % dp) * rows, out_rows, 0)
    blocks = split(grad_out, dp)[::-1]
    pieces = []
    for m in range(dp):
        pairs = {((i % dp + m) % dp) * seq + i // dp: i for i in range(count)}
        pieces.append(links.send(blocks[m], lambda i, pairs=pairs: pairs[i]))

    dq, dk, dv = attend_back(query, keys, values, slope_low, lse, place, start, length)
    unused, prepare_pull = jax.vjp(prepare, joined, query_gain, key_gain)
    slope_joined, query_gain_part, key_gain_part = prepare_pull((dq, dk, dv))
    slope_joined, pieces = lax.optimization_barrier((slope_joined.astype(BF16), pieces))
    attention_out_gradient = sum(piece.astype(F32) for piece in pieces)
    grad_in = tn(normed_all, slope_joined)
    attention_gain_part = jnp.sum(grad_in * w_in.astype(F32), axis=1) / attention_gain
    grad_in = grad_in.astype(BF16).reshape(count, rows, columns)
    sent = nt(slope_joined[middle:], w_in).astype(BF16)
    gains = jnp.concatenate([attention_gain_part, query_gain_part, key_gain_part, feed_gain_part])
    slope_first, gains = links.scatter_beside(
        nt(slope_joined[:middle], w_in), sent, links.sequence, gains.reshape(-1, 2 * HEAD_DIM), links.every
    )
    gains = gains.reshape(-1)
    grad_in = lax.all_to_all(grad_in, AXES, 0, 0, tiled=True).astype(F32)
    grad_in = jnp.sum(grad_in.reshape(dp, seq, rows, columns), axis=0)
    split_key = q_heads * HEAD_DIM
    grad_query = jnp.transpose(grad_in[:, :, :split_key], (1, 0, 2)).reshape(rows, D)
    grad_key = jnp.sum(
        grad_in[:, :, split_key : split_key + HEAD_DIM].reshape(KV_HEADS, shared, rows, HEAD_DIM), axis=1
    )
    grad_value = jnp.sum(
        grad_in[:, :, split_key + HEAD_DIM :].reshape(KV_HEADS, shared, rows, HEAD_DIM), axis=1
    )
    attention_in_gradient = jnp.concatenate(
        [
            grad_query,
            jnp.transpose(grad_key, (1, 0, 2)).reshape(rows, width),
            jnp.transpose(grad_value, (1, 0, 2)).reshape(rows, width),
        ],
        axis=1,
    )
    unused, first_pull = jax.vjp(lambda v: normalize(v, attention_gain), inputs)
    (slope_inputs,) = first_pull(slope_first)
    input_gradient = (slope_resid + slope_inputs).astype(BF16).reshape(batch, length, D)
    cut = [D, D + HEAD_DIM, D + 2 * HEAD_DIM]
    return (
        layer_output,
        input_gradient,
        gains[: cut[0]],
        attention_in_gradient,
        gains[cut[0] : cut[1]],
        gains[cut[1] : cut[2]],
        attention_out_gradient,
        gains[cut[2] :],
        feed_weight_gradient,
    )


def solution(mesh):
    tokens = P("dp", "seq", None)
    rows = P(("dp", "seq"), None)
    return jax.shard_map(
        on_device,
        mesh=mesh,
        in_specs=(tokens, P("dp", None), P(), rows, P(), P(), rows, P(), rows, tokens),
        out_specs=(tokens, tokens, P(), rows, P(), P(), rows, P(), rows),
        check_vma=False,
    )
```

```python
import functools
import math

import jax
import jax.numpy as jnp
import numpy as np
from jax import lax
from jax.experimental import pallas as pl
from jax.experimental.pallas import tpu as pltpu
from jax.sharding import PartitionSpec as P

D = 2048
HEADS = 32
KV_HEADS = 8
HEAD_DIM = 64
EPSILON = 1e-06
NEGATIVE = -1e30
AXES = ("dp", "seq")
F32 = jnp.float32
BF16 = jnp.bfloat16


def nt(left, right):
    return lax.dot_general(left, right, (((1,), (1,)), ((), ())), preferred_element_type=F32)


def nn(left, right):
    return jnp.dot(left, right, preferred_element_type=F32)


def tn(left, right):
    return lax.dot_general(left, right, (((0,), (0,)), ((), ())), preferred_element_type=F32)


def normalize(value, gain):
    return value * lax.rsqrt(jnp.mean(value * value, axis=-1, keepdims=True) + EPSILON) * gain


def rotate(value, cosine, sine):
    half = value.shape[-1] // 2
    first = value[..., :half]
    second = value[..., half:]
    return jnp.concatenate(
        [first * cosine - second * sine, second * cosine + first * sine], axis=-1
    )


class Links:
    def __init__(self, dp, seq):
        self.dp, self.seq, self.count = dp, seq, dp * seq
        plane = [1 << b for b in range(1, seq.bit_length() - 1)]
        depth = [seq << b for b in range(dp.bit_length() - 1)]
        both = lambda bits: [(bit, bit) for bit in bits]
        self.core = both([1])
        self.plane = list(zip(plane, plane[::-1]))
        self.near = both(depth[:1])
        self.sequence = self.plane + self.core
        self.tokens = both(depth[1:][::-1]) + self.plane
        self.every = both([1] + depth + plane)

    def send(self, value, target):
        return lax.ppermute(value, AXES, [(i, target(i)) for i in range(self.count)])

    def flip(self, value, level):
        return self.send(value, lambda i: i ^ level[i % 2])

    def slot_masks(self, index):
        masks = [0]
        for level in self.plane:
            masks = masks + [mask ^ level[index % 2] for mask in masks]
        other = [0]
        for level in self.plane:
            other = other + [mask ^ level[(index + 1) % 2] for mask in other]
        return masks + [mask ^ 1 for mask in other]

    def gather(self, value, levels):
        for level in levels:
            value = jnp.concatenate([value, self.flip(value, level)], axis=0)
        return value

    def scatter(self, kept, sent, levels):
        for level in levels[::-1]:
            got = self.flip(sent, level)
            half = kept.shape[0] // 2
            if level is levels[0]:
                return kept.astype(F32) + got.astype(F32)
            sent = (kept[half:].astype(F32) + got[half:].astype(F32)).astype(BF16)
            kept = kept[:half].astype(F32) + got[:half].astype(F32)

    def scatter_beside(self, kept, sent, levels, small, small_levels):
        ends = [1 + (len(small_levels) - 1) * i // (len(levels) - 1) for i in range(len(levels))]
        done = 0
        for level, end in zip(levels[::-1], ends):
            got = self.flip(sent, level)
            for small_level in small_levels[done:end]:
                small = small + self.flip(small, small_level)
            done = end
            half = kept.shape[0] // 2
            if level is levels[0]:
                return kept.astype(F32) + got.astype(F32), small
            sent = (kept[half:].astype(F32) + got[half:].astype(F32)).astype(BF16)
            kept = kept[:half].astype(F32) + got[:half].astype(F32)
            sent, small = lax.optimization_barrier((sent, small))


def attend_kernel(q_ref, k_ref, v_ref, place_ref, start_ref, key_place_ref, o_ref, lse_ref):
    heads = q_ref.shape[0]
    keys, values = k_ref[...], v_ref[...]
    key_place = key_place_ref[...]
    allowed = (key_place <= place_ref[...]) & (key_place >= start_ref[...])
    for head in range(heads):
        scores = nt(q_ref[head], keys) * HEAD_DIM ** (-0.5)
        scores = jnp.where(allowed, scores, NEGATIVE)
        top = jnp.max(scores, axis=-1, keepdims=True)
        weights = jnp.exp(scores - top)
        whole = jnp.sum(weights, axis=-1, keepdims=True)
        out = nn(weights.astype(BF16), values) / whole
        o_ref[:, head * HEAD_DIM : (head + 1) * HEAD_DIM] = out.astype(BF16)
        lse_ref[:, head : head + 1] = top + jnp.log(whole)


def attend_back_kernel(
    q_ref, k_ref, v_ref, do_ref, lse_ref, place_ref, start_ref, key_place_ref, dq_ref, dk_ref, dv_ref
):
    heads = q_ref.shape[0]
    scale = HEAD_DIM ** (-0.5)

    @pl.when(pl.program_id(0) == 0)
    def _():
        dk_ref[...] = jnp.zeros_like(dk_ref)
        dv_ref[...] = jnp.zeros_like(dv_ref)

    keys, values = k_ref[...], v_ref[...]
    key_place = key_place_ref[...]
    allowed = (key_place <= place_ref[...]) & (key_place >= start_ref[...])
    for head in range(heads):
        query = q_ref[head]
        slope = do_ref[:, head * HEAD_DIM : (head + 1) * HEAD_DIM]
        scores = jnp.where(allowed, nt(query, keys) * scale, NEGATIVE)
        chance = jnp.exp(scores - lse_ref[:, head : head + 1])
        slope_chance = nt(slope, values)
        moved = chance * slope_chance
        offset = jnp.sum(moved, axis=-1, keepdims=True)
        slope_scores = (moved - chance * offset).astype(BF16)
        dq_ref[head] = nn(slope_scores, keys) * scale
        dk_ref[...] += tn(slope_scores, query) * scale
        dv_ref[...] += tn(chance.astype(BF16), slope)


def attend(query, keys, values, place, start, block):
    heads, length, width = query.shape
    rows = pl.BlockSpec((block, 1), lambda i: (i, 0))
    whole = pl.BlockSpec((length, width), lambda i: (0, 0))
    return pl.pallas_call(
        attend_kernel,
        grid=(length // block,),
        in_specs=[
            pl.BlockSpec((heads, block, width), lambda i: (0, i, 0)),
            whole,
            whole,
            rows,
            rows,
            pl.BlockSpec((1, length), lambda i: (0, 0)),
        ],
        out_specs=[
            pl.BlockSpec((block, heads * width), lambda i: (i, 0)),
            pl.BlockSpec((block, heads), lambda i: (i, 0)),
        ],
        out_shape=[
            jax.ShapeDtypeStruct((length, heads * width), BF16),
            jax.ShapeDtypeStruct((length, heads), F32),
        ],
        cost_estimate=pl.CostEstimate(
            flops=4 * heads * length * length * 256,
            transcendentals=heads * length * length,
            bytes_accessed=8 * heads * length * width,
        ),
        name="attend",
    )(query, keys, values, place[:, None], start[:, None], place[None, :])


def attend_back(query, keys, values, slope, lse, place, start, block):
    heads, length, width = query.shape
    rows = pl.BlockSpec((block, 1), lambda i: (i, 0))
    whole = pl.BlockSpec((length, width), lambda i: (0, 0))
    byhead = pl.BlockSpec((heads, block, width), lambda i: (0, i, 0))
    return pl.pallas_call(
        attend_back_kernel,
        grid=(length // block,),
        in_specs=[
            byhead,
            whole,
            whole,
            pl.BlockSpec((block, heads * width), lambda i: (i, 0)),
            pl.BlockSpec((block, heads), lambda i: (i, 0)),
            rows,
            rows,
            pl.BlockSpec((1, length), lambda i: (0, 0)),
        ],
        out_specs=[byhead, whole, whole],
        out_shape=[
            jax.ShapeDtypeStruct((heads, length, width), F32),
            jax.ShapeDtypeStruct((length, width), F32),
            jax.ShapeDtypeStruct((length, width), F32),
        ],
        cost_estimate=pl.CostEstimate(
            flops=10 * heads * length * length * 256,
            transcendentals=heads * length * length,
            bytes_accessed=16 * heads * length * width,
        ),
        name="attend_back",
    )(query, keys, values, slope, lse, place[:, None], start[:, None], place[None, :])


def split(value, count):
    size = value.shape[0] // count
    return [value[i * size : (i + 1) * size] for i in range(count)]


def feed(normed, slope, gate_up, down):
    both = nt(normed, gate_up)
    hidden_count = down.shape[0]
    gate, up = both[:, :hidden_count], both[:, hidden_count:]
    slope_hidden = nt(slope, down)
    bend = jax.nn.sigmoid(gate)
    curve = gate * bend
    hidden = (curve * up).astype(BF16)
    slope_gate = (slope_hidden * up * (bend * (1.0 + gate * (1.0 - bend)))).astype(BF16)
    slope_up = (slope_hidden * curve).astype(BF16)
    slope_both = jnp.concatenate([slope_gate, slope_up], axis=1)
    return hidden, slope_both


def on_device(
    layer_input,
    document_lengths,
    attention_gain,
    attention_in,
    query_gain,
    key_gain,
    attention_out,
    feed_gain,
    feed_weight,
    cotangent,
):
    dp, seq = lax.axis_size("dp"), lax.axis_size("seq")
    links = Links(dp, seq)
    count = links.count
    batch, length = layer_input.shape[0], layer_input.shape[1]
    tokens = batch * length
    here_dp, here = lax.axis_index("dp"), lax.axis_index("seq")
    q_heads = HEADS // seq
    shared = seq // KV_HEADS
    width = KV_HEADS * HEAD_DIM
    rows = attention_in.shape[0]

    masks = jnp.asarray(np.array([links.slot_masks(0), links.slot_masks(1)], np.int32))
    slot_seq = here ^ jnp.where(here % 2 == 0, masks[0], masks[1])
    place = (slot_seq[:, None] * length + jnp.arange(length)[None, :]).reshape(-1)
    lengths = document_lengths[0]
    ends = jnp.cumsum(lengths)
    start = jnp.sum(jnp.where(place[:, None] >= ends[None, :], lengths[None, :], 0), axis=1)
    half = HEAD_DIM // 2
    frequency = jnp.exp(jnp.arange(half).astype(F32) * (-2.0 * math.log(10000.0) / HEAD_DIM))
    angles = (place - start).astype(F32)[:, None] * frequency
    cosine, sine = jnp.cos(angles), jnp.sin(angles)

    w_query = attention_in[:, :D].reshape(rows, seq, q_heads * HEAD_DIM)
    w_key = attention_in[:, D : D + width].reshape(rows, KV_HEADS, HEAD_DIM)
    w_value = attention_in[:, D + width :].reshape(rows, KV_HEADS, HEAD_DIM)
    w_mine = jnp.concatenate(
        [w_query, jnp.repeat(w_key, shared, axis=1), jnp.repeat(w_value, shared, axis=1)], axis=2
    )
    w_mine = jnp.transpose(w_mine, (1, 0, 2))
    columns = w_mine.shape[2]
    w_in = lax.all_to_all(
        jnp.broadcast_to(w_mine[None], (dp,) + w_mine.shape).reshape(count, rows, columns),
        AXES, 0, 0, tiled=True,
    ).reshape(D, columns)

    w_slots = [
        links.send(attention_out, lambda i, m=m: ((i % dp + m) % dp) * seq + i // dp)
        for m in range(dp)
    ]
    w_out = jnp.concatenate(w_slots[::-1] + w_slots[::-1], axis=0)
    out_rows = dp * rows
    w_out = lax.dynamic_slice_in_dim(w_out, ((dp - 1 - here_dp) % dp) * rows, out_rows, 0)

    inputs = layer_input.astype(F32).reshape(tokens, D)
    normed = normalize(inputs, attention_gain).astype(BF16)
    normed_all = links.gather(normed, links.sequence)
    joined = nn(normed_all, w_in)
    whole = normed_all.shape[0]

    def prepare(joined, query_gain, key_gain):
        split_key = q_heads * HEAD_DIM
        query = joined[:, :split_key].reshape(whole, q_heads, HEAD_DIM)
        keys = joined[:, split_key : split_key + HEAD_DIM]
        values = joined[:, split_key + HEAD_DIM :]
        query = rotate(normalize(query, query_gain), cosine[:, None], sine[:, None])
        keys = rotate(normalize(keys, key_gain), cosine, sine)
        return jnp.transpose(query, (1, 0, 2)), keys, values

    query, keys, values = prepare(joined, query_gain, key_gain)
    query, keys, values = query.astype(BF16), keys.astype(BF16), values.astype(BF16)
    slope_out = cotangent.reshape(tokens, D)
    first_levels, last_level = links.tokens[:-1], links.tokens[-1]
    slope_first_half = links.gather(slope_out, first_levels)
    query, keys, values, slope_first_half = lax.optimization_barrier(
        (query, keys, values, slope_first_half)
    )
    attended, lse = attend(query, keys, values, place, start, length)
    middle = whole // 2
    sent = nn(attended[middle:], w_out).astype(BF16)
    branch = links.scatter(nn(attended[:middle], w_out), sent, links.sequence)
    resid = inputs + branch
    normed_feed = normalize(resid, feed_gain).astype(BF16)

    near = links.flip(feed_weight, links.near[0])
    shares = [feed_weight, near, links.flip(feed_weight, links.core[0]), links.flip(near, links.core[0])]
    gate_up = jnp.concatenate(
        [share[:, :D] for share in shares] + [share[:, D : 2 * D] for share in shares], axis=0
    )
    down = jnp.concatenate([share[:, 2 * D :] for share in shares], axis=0)
    units = down.shape[0]
    slope_last_half = links.flip(slope_first_half, last_level)
    low_first = links.gather(normed_feed, first_levels)
    low_last = links.flip(low_first, last_level)
    hidden_first, both_first = feed(low_first, slope_first_half, gate_up, down)
    hidden_last, both_last = feed(low_last, slope_last_half, gate_up, down)
    sent = nn(both_last, gate_up).astype(BF16)
    slope_normed = links.scatter(nn(both_first, gate_up), sent, links.tokens)
    unused, norm_pull = jax.vjp(normalize, resid, feed_gain)
    slope_resid, feed_gain_part = norm_pull(slope_normed)
    slope_resid = slope_resid + slope_out.astype(F32)
    slope_branch = slope_resid.astype(BF16)

    grad_both = tn(both_first, low_first) + tn(both_last, low_last)
    grad_down = tn(hidden_first, slope_first_half) + tn(hidden_last, slope_last_half)
    parts = []
    for part in (grad_both[:units], grad_both[units:], grad_down):
        parts.append(
            links.scatter(part[: units // 2], part[units // 2 :].astype(BF16), links.near + links.core)
        )
    feed_weight_gradient = jnp.concatenate(parts, axis=1)

    hidden_first, hidden_last, slope_branch = lax.optimization_barrier(
        (hidden_first, hidden_last, slope_branch)
    )
    mixed = links.scatter(
        nn(hidden_first, down), nn(hidden_last, down).astype(BF16), links.tokens
    )

    slope_branch_all = links.gather(slope_branch, links.sequence)
    slope_low = nt(slope_branch_all, w_out).astype(BF16)
    grad_out = tn(attended, slope_branch_all).astype(BF16)
    grad_out = jnp.concatenate([grad_out, grad_out], axis=0)
    grad_out = lax.dynamic_slice_in_dim(grad_out, ((here_dp + 1) % dp) * rows, out_rows, 0)
    grad_out, slope_low = lax.optimization_barrier((grad_out, slope_low))
    blocks = split(grad_out, dp)[::-1]
    pieces = []
    for m in range(dp):
        pairs = {((i % dp + m) % dp) * seq + i // dp: i for i in range(count)}
        pieces.append(links.send(blocks[m], lambda i, pairs=pairs: pairs[i]))

    dq, dk, dv = attend_back(query, keys, values, slope_low, lse, place, start, length)
    dq, dk, dv, pieces = lax.optimization_barrier((dq, dk, dv, pieces))
    unused, prepare_pull = jax.vjp(prepare, joined, query_gain, key_gain)
    slope_joined, query_gain_part, key_gain_part = prepare_pull((dq, dk, dv))
    slope_joined, mixed = lax.optimization_barrier((slope_joined.astype(BF16), mixed))
    layer_output = (resid + mixed).astype(BF16).reshape(batch, length, D)
    attention_out_gradient = sum(piece.astype(F32) for piece in pieces)
    grad_in = tn(normed_all, slope_joined)
    attention_gain_part = jnp.sum(grad_in * w_in.astype(F32), axis=1) / attention_gain
    grad_in = grad_in.astype(BF16).reshape(count, rows, columns)
    sent = nt(slope_joined[middle:], w_in).astype(BF16)
    gains = jnp.concatenate([attention_gain_part, query_gain_part, key_gain_part, feed_gain_part])
    slope_first, gains = links.scatter_beside(
        nt(slope_joined[:middle], w_in), sent, links.sequence, gains.reshape(-1, 2 * HEAD_DIM), links.every
    )
    gains = gains.reshape(-1)
    grad_in = lax.all_to_all(grad_in, AXES, 0, 0, tiled=True).astype(F32)
    grad_in = jnp.sum(grad_in.reshape(dp, seq, rows, columns), axis=0)
    split_key = q_heads * HEAD_DIM
    grad_query = jnp.transpose(grad_in[:, :, :split_key], (1, 0, 2)).reshape(rows, D)
    grad_key = jnp.sum(
        grad_in[:, :, split_key : split_key + HEAD_DIM].reshape(KV_HEADS, shared, rows, HEAD_DIM), axis=1
    )
    grad_value = jnp.sum(
        grad_in[:, :, split_key + HEAD_DIM :].reshape(KV_HEADS, shared, rows, HEAD_DIM), axis=1
    )
    attention_in_gradient = jnp.concatenate(
        [
            grad_query,
            jnp.transpose(grad_key, (1, 0, 2)).reshape(rows, width),
            jnp.transpose(grad_value, (1, 0, 2)).reshape(rows, width),
        ],
        axis=1,
    )
    unused, first_pull = jax.vjp(lambda v: normalize(v, attention_gain), inputs)
    (slope_inputs,) = first_pull(slope_first)
    input_gradient = (slope_resid + slope_inputs).astype(BF16).reshape(batch, length, D)
    cut = [D, D + HEAD_DIM, D + 2 * HEAD_DIM]
    return (
        layer_output,
        input_gradient,
        gains[: cut[0]],
        attention_in_gradient,
        gains[cut[0] : cut[1]],
        gains[cut[1] : cut[2]],
        attention_out_gradient,
        gains[cut[2] :],
        feed_weight_gradient,
    )


def solution(mesh):
    tokens = P("dp", "seq", None)
    rows = P(("dp", "seq"), None)
    return jax.shard_map(
        on_device,
        mesh=mesh,
        in_specs=(tokens, P("dp", None), P(), rows, P(), P(), rows, P(), rows, tokens),
        out_specs=(tokens, tokens, P(), rows, P(), P(), rows, P(), rows),
        check_vma=False,
    )
```
